32 devices in a mesh: dp: 16 (over z, y, x), mp: 2 (over core).
Axes of the slice: x: 2, y: 2, z: 4, core: 2. Of those that a mesh axis runs over, the one named last changes fastest.
Arguments:
- hidden: bfloat16 [2048, 4096], P('dp', 'mp'), may hold values from -6 to 6
- attended: bfloat16 [2048, 4096], P('dp', 'mp'), may hold values from -6 to 6
- query_cotangent: bfloat16 [2048, 4096], P('dp', 'mp'), may hold values from -1.5 to 1.5
- output_cotangent: bfloat16 [2048, 4096], P('dp', 'mp'), may hold values from -1.5 to 1.5
- query_projection_weight: bfloat16 [4096, 4096], P('dp', 'mp'), may hold values from -0.09375 to 0.09375
- output_projection_weight: bfloat16 [4096, 4096], P('dp', 'mp'), may hold values from -0.09375 to 0.09375
- narrower: bfloat16 [256, 16, 4096], P('dp', None, 'mp'), may hold values from -0.09375 to 0.09375
- widener: bfloat16 [256, 16, 4096], P('dp', None, 'mp'), may hold values from -0.375 to 0.375
- reducer: bfloat16 [256, 16, 4096], P('dp', None, 'mp'), may hold values from -0.09375 to 0.09375
- enlarger: bfloat16 [256, 16, 4096], P('dp', None, 'mp'), may hold values from -0.375 to 0.375
- block_adapter: int32 [512], P('dp'), may hold values from 0 to 255, as said below
- block_fill: int32 [512], P('dp'), may hold values from 1 to 4
Outputs:
- queries: bfloat16 [2048, 4096], P('dp', 'mp')
- projected: bfloat16 [2048, 4096], P('dp', 'mp')
- hidden_state_gradient: bfloat16 [2048, 4096], P('dp', 'mp')
- attention_output_gradient: bfloat16 [2048, 4096], P('dp', 'mp')
- narrower_gradient: float32 [256, 16, 4096], P('dp', None, 'mp')
- widener_gradient: float32 [256, 16, 4096], P('dp', None, 'mp')
- reducer_gradient: float32 [256, 16, 4096], P('dp', None, 'mp')
- enlarger_gradient: float32 [256, 16, 4096], P('dp', None, 'mp')
The draws below stay inside these ranges and needn't reach their ends.
Inputs may be any that keep to these rules, and one draw needn't show every extreme that they name: `block_adapter`: the owner of adapter e is e // 16. Among the 32 blocks of one group (one index of dp), at most 2 have adapters of one owner, and some owner has exactly 2 blocks in every group.
All inputs are finite; a program needn't handle non-finite values.
Results may differ from the reference program's by a relative error of at most 0.015.
Values may be sent and summed in bfloat16 or wider, within the bound.
A program may use at most 128 MiB of HBM per device.

```python
import jax
import jax.numpy as jnp
from jax import lax

MODEL_FEATURES = 4096
QUERY_FEATURES = 4096
RANK = 16
ADP_DEV = 16
GROUP_TOKENS = 128
BLOCK = 4
TOKEN_SLOTS = 2048
ADAPTERS = 256
BLOCKS = 512
N_DP = 16
N_MP = 2


def draw_block_adapter(key, part):
    groups = ADAPTERS // ADP_DEV
    per_group = GROUP_TOKENS // BLOCK
    slots = (per_group + groups - 1) // groups
    hot_key, group_key, local_key = jax.random.split(jax.random.fold_in(key, 7), 3)
    hottest = jax.random.randint(hot_key, (), 0, groups)

    def one_group(group_seed):
        perm_key, order_key = jax.random.split(group_seed)
        entries = jax.random.permutation(perm_key, (groups - 1) * slots)[:per_group - slots]
        others = (entries // slots).astype(jnp.int32)
        others = others + (others >= hottest).astype(jnp.int32)
        owners = jnp.concatenate([jnp.full((slots,), hottest, jnp.int32), others])
        return jax.random.permutation(order_key, owners)
    owners = jax.vmap(one_group)(jax.random.split(group_key, groups))
    local = jax.random.randint(local_key, (groups, per_group), 0, ADP_DEV)
    return (owners * ADP_DEV + local).reshape(-1).astype(jnp.int32)


def touch_ends(array, stream_key, least, top_value):
    dims = array.shape
    index_at = [jax.random.randint(jax.random.fold_in(stream_key, axis), (), 0, dims[axis]) for axis in range(len(dims))]
    array = array.at[tuple(index_at)].set(least)
    longest = dims.index(max(dims))
    index_at[longest] = (index_at[longest] + 1) % dims[longest]
    return array.at[tuple(index_at)].set(top_value)


def level_of(key, dims, cuts, low, largest):
    level = 1.0
    for axis_at, parts in cuts:
        draws = jax.random.uniform(jax.random.fold_in(jax.random.fold_in(key, 6), axis_at), (parts,), jnp.float32, low / len(cuts), largest / len(cuts))
        level = level * jnp.repeat(jnp.exp(draws), dims[axis_at] // parts).reshape((-1,) + (1,) * (len(dims) - 1 - axis_at))
    return level


def gaussian(stream_key, shape, spread, reach, cuts=(), kind=jnp.bfloat16):
    level = level_of(stream_key, shape, cuts, -0.22, 0.18) if cuts else 1.0
    result = jax.random.normal(stream_key, shape, jnp.float32) * spread * level
    return jnp.minimum(jnp.maximum(result, -reach), reach).astype(kind)


def setup_inputs(seed: int = 0) -> dict:
    keys = jax.random.split(jax.random.key(seed), 13)
    return {
        "hidden": gaussian(keys[0], (TOKEN_SLOTS, MODEL_FEATURES), 1.0, 6.0, ((0, 16), (1, 2))),
        "attended": gaussian(keys[1], (TOKEN_SLOTS, QUERY_FEATURES), 1.0, 6.0, ((0, 16), (1, 2))),
        "query_cotangent": gaussian(keys[2], (TOKEN_SLOTS, QUERY_FEATURES), 0.25, 1.5, ((0, 16), (1, 2))),
        "output_cotangent": gaussian(keys[3], (TOKEN_SLOTS, MODEL_FEATURES), 0.25, 1.5, ((0, 16), (1, 2))),
        "query_projection_weight": gaussian(keys[4], (MODEL_FEATURES, QUERY_FEATURES), MODEL_FEATURES ** -0.5, 0.09375, ((0, 16), (1, 2))),
        "output_projection_weight": gaussian(keys[5], (QUERY_FEATURES, MODEL_FEATURES), QUERY_FEATURES ** -0.5, 0.09375, ((0, 16), (1, 2))),
        "narrower": gaussian(keys[6], (ADAPTERS, RANK, MODEL_FEATURES), MODEL_FEATURES ** -0.5, 0.09375, ((0, 16), (2, 2))),
        "widener": gaussian(keys[7], (ADAPTERS, RANK, QUERY_FEATURES), (16 * RANK) ** -0.5, 0.375, ((0, 16), (2, 2))),
        "reducer": gaussian(keys[8], (ADAPTERS, RANK, QUERY_FEATURES), QUERY_FEATURES ** -0.5, 0.09375, ((0, 16), (2, 2))),
        "enlarger": gaussian(keys[9], (ADAPTERS, RANK, MODEL_FEATURES), (16 * RANK) ** -0.5, 0.375, ((0, 16), (2, 2))),
        "block_adapter": draw_block_adapter(jax.random.fold_in(keys[12], 71), 0),
        "block_fill": touch_ends(jax.random.randint(keys[11], (BLOCKS,), 1, BLOCK + 1), jax.random.fold_in(keys[11], 1), 1, BLOCK).astype(jnp.int32),
    }


adapter_scale = 2.0


def batched_result(form, left, right):
    return jnp.einsum(form, left.astype(jnp.float32), right.astype(jnp.float32), precision=lax.Precision.HIGHEST)


def reference(hidden, attended, query_cotangent, output_cotangent, query_projection_weight, output_projection_weight, narrower, widener, reducer, enlarger, block_adapter, block_fill):
    per_group = GROUP_TOKENS // BLOCK
    row_ids = lax.broadcasted_iota(jnp.int32, (BLOCKS, BLOCK), 1)
    live = (row_ids < block_fill[:, None]).astype(jnp.bfloat16).reshape(TOKEN_SLOTS, 1)
    query_masked = query_cotangent * live
    output_masked = output_cotangent * live

    def per_group_work(inputs):
        hid, att, qcot, ocot, ids = inputs
        hidden_block_list = hid.reshape(per_group, BLOCK, MODEL_FEATURES)
        attended_block_list = att.reshape(per_group, BLOCK, QUERY_FEATURES)
        query_cotangent_blocks = qcot.reshape(per_group, BLOCK, QUERY_FEATURES)
        output_cotangent_blocks = ocot.reshape(per_group, BLOCK, MODEL_FEATURES)
        query_down_factor = narrower[ids]
        query_up_factor = widener[ids]
        output_down_factor = reducer[ids]
        output_up_factor = enlarger[ids]
        query_rank_rows = batched_result("brf,bkf->brk", hidden_block_list, query_down_factor).astype(jnp.bfloat16)
        output_rank_rows = batched_result("brf,bkf->brk", attended_block_list, output_down_factor).astype(jnp.bfloat16)
        query_backward_pass = batched_result("brf,bkf->brk", query_cotangent_blocks, query_up_factor).astype(jnp.bfloat16)
        output_backward_pass = batched_result("brf,bkf->brk", output_cotangent_blocks, output_up_factor).astype(jnp.bfloat16)
        query_adapter_term = (adapter_scale * batched_result("ixa,iaq->ixq", query_rank_rows, query_up_factor)).astype(jnp.bfloat16)
        output_adapter_term = (adapter_scale * batched_result("ixa,iaq->ixq", output_rank_rows, output_up_factor)).astype(jnp.bfloat16)
        hidden_adapter_term = (adapter_scale * batched_result("ixa,iaq->ixq", query_backward_pass, query_down_factor)).astype(jnp.bfloat16)
        attended_adapter_term = (adapter_scale * batched_result("ixa,iaq->ixq", output_backward_pass, output_down_factor)).astype(jnp.bfloat16)
        query_down_gradient = adapter_scale * batched_result("iot,iol->itl", query_backward_pass, hidden_block_list)
        query_up_gradient = adapter_scale * batched_result("iot,iol->itl", query_rank_rows, query_cotangent_blocks)
        output_down_gradient = adapter_scale * batched_result("iot,iol->itl", output_backward_pass, attended_block_list)
        output_up_gradient = adapter_scale * batched_result("iot,iol->itl", output_rank_rows, output_cotangent_blocks)
        return (query_adapter_term.reshape(GROUP_TOKENS, QUERY_FEATURES), output_adapter_term.reshape(GROUP_TOKENS, MODEL_FEATURES),
                hidden_adapter_term.reshape(GROUP_TOKENS, MODEL_FEATURES), attended_adapter_term.reshape(GROUP_TOKENS, QUERY_FEATURES),
                query_down_gradient, query_up_gradient, output_down_gradient, output_up_gradient)

    result_list = lax.map(per_group_work, (hidden.reshape(N_DP, GROUP_TOKENS, MODEL_FEATURES), attended.reshape(N_DP, GROUP_TOKENS, QUERY_FEATURES),
                                       query_masked.reshape(N_DP, GROUP_TOKENS, QUERY_FEATURES), output_masked.reshape(N_DP, GROUP_TOKENS, MODEL_FEATURES),
                                       block_adapter.reshape(N_DP, per_group)))
    query_adapter_term = result_list[0].reshape(TOKEN_SLOTS, QUERY_FEATURES)
    output_adapter_term = result_list[1].reshape(TOKEN_SLOTS, MODEL_FEATURES)
    hidden_adapter_term = result_list[2].reshape(TOKEN_SLOTS, MODEL_FEATURES)
    attended_adapter_term = result_list[3].reshape(TOKEN_SLOTS, QUERY_FEATURES)

    def collect(grads, width):
        return jax.ops.segment_sum(grads.reshape(BLOCKS, RANK, width), block_adapter, num_segments=ADAPTERS)

    narrower_gradient = collect(result_list[4], MODEL_FEATURES)
    widener_gradient = collect(result_list[5], QUERY_FEATURES)
    reducer_gradient = collect(result_list[6], QUERY_FEATURES)
    enlarger_gradient = collect(result_list[7], MODEL_FEATURES)

    queries = (jnp.dot(hidden, query_projection_weight, preferred_element_type=jnp.float32) + query_adapter_term.astype(jnp.float32)).astype(jnp.bfloat16)
    projected = (jnp.dot(attended, output_projection_weight, preferred_element_type=jnp.float32) + output_adapter_term.astype(jnp.float32)).astype(jnp.bfloat16)

    query_cols = QUERY_FEATURES // N_MP
    output_cols = MODEL_FEATURES // N_MP
    hidden_total_sum = jnp.zeros((TOKEN_SLOTS, MODEL_FEATURES), jnp.float32)
    attended_total_sum = jnp.zeros((TOKEN_SLOTS, QUERY_FEATURES), jnp.float32)
    for index in range(N_MP):
        part = lax.dot_general(query_masked[:, index * query_cols:(index + 1) * query_cols],
                               query_projection_weight[:, index * query_cols:(index + 1) * query_cols],
                               (((1,), (1,)), ((), ())), preferred_element_type=jnp.float32)
        hidden_total_sum = hidden_total_sum + lax.optimization_barrier(part.astype(jnp.bfloat16)).astype(jnp.float32)
        other = lax.dot_general(output_masked[:, index * output_cols:(index + 1) * output_cols],
                                output_projection_weight[:, index * output_cols:(index + 1) * output_cols],
                                (((1,), (1,)), ((), ())), preferred_element_type=jnp.float32)
        attended_total_sum = attended_total_sum + lax.optimization_barrier(other.astype(jnp.bfloat16)).astype(jnp.float32)
    hidden_state_gradient = (hidden_total_sum + hidden_adapter_term.astype(jnp.float32)).astype(jnp.bfloat16)
    attention_output_gradient = (attended_total_sum + attended_adapter_term.astype(jnp.float32)).astype(jnp.bfloat16)
    return (queries, projected, hidden_state_gradient, attention_output_gradient,
            narrower_gradient, widener_gradient, reducer_gradient, enlarger_gradient)
```

```python
import jax
import jax.numpy as jnp
from jax import lax
from jax.sharding import Mesh, PartitionSpec as P

adapter_scale = 2.0


def product(left, right, contract):
    return lax.dot_general(
        left, right, ((contract[:1], contract[1:]), ((), ())), preferred_element_type=jnp.float32
    )


def one_hot(condition):
    return condition.astype(jnp.bfloat16)


def iota(shape, dimension):
    return lax.broadcasted_iota(jnp.int32, shape, dimension)


def stacked_columns(values, parts):
    wide = values.shape[1] // parts
    return jnp.concatenate([values[:, i * wide : (i + 1) * wide] for i in range(parts)], axis=0)


def unstacked_columns(values, parts):
    rows = values.shape[0] // parts
    return jnp.concatenate([values[i * rows : (i + 1) * rows] for i in range(parts)], axis=1)


def exchange(values, axis):
    return lax.all_to_all(values, axis, split_axis=0, concat_axis=0, tiled=True)


def on_device(
    hidden,
    attended,
    query_cotangent,
    output_cotangent,
    query_projection_weight,
    output_projection_weight,
    narrower,
    widener,
    reducer,
    enlarger,
    block_adapter,
    block_fill,
):
    dp = ("far", "near")
    far = lax.axis_size("far")
    owners = far * lax.axis_size("near")
    tokens = hidden.shape[0]
    group_blocks = block_adapter.shape[0]
    width = tokens // group_blocks
    capacity = -(-group_blocks // owners)
    per_owner, rank = narrower.shape[:2]
    lanes = -(-per_owner // 128) * 128

    query_rows = lax.all_gather(query_projection_weight, "near", axis=0, tiled=True)
    output_rows = lax.all_gather(output_projection_weight, "near", axis=0, tiled=True)

    row_ids = iota((group_blocks, width), 1)
    live = one_hot(row_ids < block_fill[:, None]).reshape(tokens, 1)
    query_masked = query_cotangent * live
    output_masked = output_cotangent * live

    owner_of = block_adapter // per_owner
    later_ids = iota((group_blocks, group_blocks), 0)
    earlier_ids = iota((group_blocks, group_blocks), 1)
    before = (owner_of[:, None] == owner_of[None, :]) & (earlier_ids < later_ids)
    position = jnp.sum(before.astype(jnp.int32), axis=1)
    slot_of = owner_of * capacity + position
    row_of = (slot_of[:, None] * width + row_ids).reshape(1, tokens)
    table = one_hot(iota((owners * capacity * width, tokens), 0) == row_of)
    local_of = jnp.broadcast_to((block_adapter % per_owner)[:, None], (group_blocks, width))
    local_hot = one_hot(iota((tokens, lanes), 1) == local_of.reshape(tokens, 1))
    sent = jnp.concatenate(
        [
            product(table, part, (1, 0)).astype(jnp.bfloat16)
            for part in (local_hot, hidden, attended, query_masked, output_masked)
        ],
        axis=1,
    )
    received = exchange(sent, dp)
    model, query = hidden.shape[1], attended.shape[1]
    ends = [lanes, lanes + model, lanes + model + query, lanes + model + 2 * query]
    hot, hid, att, qcot, ocot = jnp.split(received, ends, axis=1)

    many = per_owner * rank
    spread = one_hot(iota((lanes, many), 0) == iota((lanes, many), 1) // rank)
    own = product(hot, spread, (1, 0))
    fold = one_hot(iota((many, rank), 0) % rank == iota((many, rank), 1))
    factors = [f.reshape(many, f.shape[2]) for f in (narrower, reducer, widener, enlarger)]
    folded = jnp.concatenate(
        [
            product((product(x, f, (1, 1)) * own).astype(jnp.bfloat16), fold, (1, 0))
            for x, f in zip((hid, att, qcot, ocot), factors)
        ],
        axis=1,
    ).astype(jnp.bfloat16)
    ranks = lax.psum(folded, "mp")
    query_rank, output_rank, query_back, output_back = [
        (product(ranks[:, i * rank : (i + 1) * rank], fold, (1, 1)) * own).astype(jnp.bfloat16)
        for i in range(4)
    ]
    down_query, down_output, up_query, up_output = factors
    returned = exchange(
        jnp.concatenate(
            [
                (adapter_scale * product(r, f, (1, 0))).astype(jnp.bfloat16)
                for r, f in (
                    (query_rank, up_query),
                    (output_rank, up_output),
                    (query_back, down_query),
                    (output_back, down_output),
                )
            ],
            axis=1,
        ),
        dp,
    )

    def gradient(ranks, rows, like):
        return (adapter_scale * product(ranks, rows, (0, 0))).reshape(like.shape)

    narrower_gradient = gradient(query_back, hid, narrower)
    widener_gradient = gradient(query_rank, qcot, widener)
    reducer_gradient = gradient(output_back, att, reducer)
    enlarger_gradient = gradient(output_rank, ocot, enlarger)

    hid_full = lax.all_gather(hidden, "mp", axis=1, tiled=True)
    att_full = lax.all_gather(attended, "mp", axis=1, tiled=True)
    depth = hid_full.shape[1] // far
    inputs = exchange(
        jnp.concatenate(
            [stacked_columns(hid_full, far), stacked_columns(att_full, far)], axis=1
        ),
        "far",
    )
    cotangents = [
        lax.all_gather(masked, "far", axis=0, tiled=True)
        for masked in (query_masked, output_masked)
    ]

    def forward(values, weight):
        part = product(values, weight, (1, 0)).astype(jnp.bfloat16)
        parts = exchange(part, "far").reshape(far, tokens, weight.shape[1])
        return jnp.sum(parts.astype(jnp.float32), axis=0)

    def backward(masked, weight):
        part = product(masked, weight, (1, 1)).astype(jnp.bfloat16)
        whole = unstacked_columns(exchange(part, "far"), far)
        return lax.psum_scatter(whole, "mp", scatter_dimension=1, tiled=True)

    base = [
        forward(inputs[:, :depth], query_rows),
        forward(inputs[:, depth:], output_rows),
        backward(cotangents[0], query_rows).astype(jnp.float32),
        backward(cotangents[1], output_rows).astype(jnp.float32),
    ]
    starts = [query, query + model, query + 2 * model]
    adapter_terms = [product(table, part, (0, 0)) for part in jnp.split(returned, starts, axis=1)]
    queries, projected, hidden_state_gradient, attention_output_gradient = [
        (b + t).astype(jnp.bfloat16) for b, t in zip(base, adapter_terms)
    ]
    return (
        queries,
        projected,
        hidden_state_gradient,
        attention_output_gradient,
        narrower_gradient,
        widener_gradient,
        reducer_gradient,
        enlarger_gradient,
    )


def solution(mesh):
    count = mesh.shape["dp"]
    far = 1
    while far * far < count or count % far:
        far += 1
    split = Mesh(
        mesh.devices.reshape(far, count // far, mesh.shape["mp"]), ("far", "near", "mp")
    )
    dp = ("far", "near")
    rows, factors = P(dp, "mp"), P(dp, None, "mp")
    return jax.shard_map(
        on_device,
        mesh=split,
        in_specs=(rows,) * 6 + (factors,) * 4 + (P(dp),) * 2,
        out_specs=(rows,) * 4 + (factors,) * 4,
        check_vma=False,
    )
```

```python
import jax
import jax.numpy as jnp
from jax import lax
from jax.experimental import pallas as pl
from jax.experimental.pallas import tpu as pltpu
from jax.sharding import Mesh, PartitionSpec as P

adapter_scale = 2.0


def product(left, right, contract):
    return lax.dot_general(
        left, right, ((contract[:1], contract[1:]), ((), ())), preferred_element_type=jnp.float32
    )


def one_hot(condition):
    return condition.astype(jnp.bfloat16)


def iota(shape, dimension):
    return lax.broadcasted_iota(jnp.int32, shape, dimension)


def block(ref, index, rows):
    return ref.at[pl.ds(pl.multiple_of(index * rows, rows), rows)]


class Place:
    def __init__(self):
        self.far, self.near, self.mp = [lax.axis_index(n) for n in ("far", "near", "mp")]
        self.fars, self.nears, self.mps = [lax.axis_size(n) for n in ("far", "near", "mp")]
        self.owner = self.far * self.nears + self.near
        self.owners = self.fars * self.nears

    def near_peers(self):
        for step in range(self.nears):
            near = lax.rem(self.near + step, self.nears)
            yield near, (self.far, near, self.mp), step == 0

    def far_peers(self):
        for step in range(self.fars):
            far = lax.rem(self.far + step, self.fars)
            yield far, (far, self.near, self.mp), step == 0

    def owner_peers(self):
        for step in range(self.owners):
            owner = lax.rem(self.owner + step, self.owners)
            yield owner, (owner // self.nears, lax.rem(owner, self.nears), self.mp), step == 0

    def skips(self, lane):
        own_half = self.far // (self.fars // self.mps) == self.mp
        return jnp.logical_and(own_half, self.far == lane)

    def greet(self):
        others = [device for _, device, own in self.owner_peers() if not own]
        for shift in range(1, self.mps):
            mp = lax.rem(self.mp + shift, self.mps)
            others += [(far, self.near, mp) for far in range(self.fars)]
        barrier = pltpu.get_barrier_semaphore()
        for device in others:
            pl.semaphore_signal(
                barrier, inc=1, device_id=device, device_id_type=pl.DeviceIdType.MESH
            )
        pl.semaphore_wait(barrier, len(others))


def both(condition, remote, local):
    if condition is True:
        local()
    elif condition is False:
        remote()
    else:
        pl.when(jnp.logical_not(condition))(remote)
        pl.when(condition)(local)


def transfer(plan, arrays, out_shapes, chunks, sends, collective_id):
    count, groups = len(arrays), len(chunks)

    def kernel(*refs):
        ins, outs = refs[:count], refs[count : count + groups]
        held = refs[count + groups : count + 2 * groups]
        send_sem, recv_sem, own_sem = refs[count + 2 * groups :]
        place = Place()
        place.greet()
        routes = list(plan(place, ins, outs))

        def remote(at, landing):
            _, source, target, device = routes[at][:4]
            return pltpu.make_async_remote_copy(
                src_ref=source,
                dst_ref=target,
                send_sem=send_sem.at[at],
                recv_sem=recv_sem.at[landing],
                device_id=device,
                device_id_type=pl.DeviceIdType.MESH,
            )

        def inward(at):
            group, source = routes[at][:2]
            return pltpu.make_async_copy(source, held[group], own_sem.at[group])

        def outward(at):
            group, _, target = routes[at][:3]
            return pltpu.make_async_copy(held[group], target, own_sem.at[group])

        def nothing():
            pass

        members = {}
        for at, route in enumerate(routes):
            members.setdefault(route[0], []).append(at)
        for at, (group, _, _, _, own, lane, _) in enumerate(routes):
            group_routes = members[group]
            stride = group_routes[-1] - group_routes[-2]
            landing = at if lane is None else group_routes[0] + lane * stride
            both(own, lambda: remote(at, landing).start(), lambda: inward(at).start())
        for at, route in enumerate(routes):

            def pass_on():
                inward(at).wait()
                outward(at).start()

            both(route[4], nothing, pass_on)
        for at, (_, _, _, _, own, _, absent) in enumerate(routes):
            both(own, lambda: remote(at, at).wait_send(), lambda: outward(at).wait())
            both(absent, lambda: remote(at, at).wait_recv(), nothing)

    anywhere = pl.BlockSpec(memory_space=pl.ANY)
    return pl.pallas_call(
        kernel,
        out_shape=[jax.ShapeDtypeStruct(shape, jnp.bfloat16) for shape in out_shapes],
        in_specs=[anywhere] * count,
        out_specs=[anywhere] * groups,
        scratch_shapes=[pltpu.VMEM(shape, jnp.bfloat16) for shape in chunks]
        + [pltpu.SemaphoreType.DMA((sends,))] * 2
        + [pltpu.SemaphoreType.DMA((groups,))],
        compiler_params=pltpu.CompilerParams(
            collective_id=collective_id, has_side_effects=True
        ),
    )(*arrays)


def distribute(place, ins, outs):
    slots, first, second, hidden, attended, query, output = ins
    tokens, rows = hidden.shape[0], first.shape[0]
    depth = outs[3].shape[1]
    each = place.fars // place.mps
    for near, device, own in place.near_peers():
        for group, weight in ((1, first), (2, second)):
            yield group, weight, block(outs[group], place.near, rows), device, own, None, own
    for shift in range(place.mps):
        mp = lax.rem(place.mp + shift, place.mps)
        for at in range(each):
            far = place.mp * each + at
            own = False if shift else far == place.far
            absent = place.skips(shift * each + at)
            for group, values in ((3, hidden), (4, attended)):
                columns = values.at[:, pl.ds(at * depth, depth)]
                target = block(outs[group], place.far, tokens)
                device = (far, place.near, mp)
                yield group, columns, target, device, own, place.far, absent
    for far, device, own in place.far_peers():
        for group, values in ((5, query), (6, output)):
            target = block(outs[group], place.far, tokens)
            yield group, values, target, device, own, None, own
    for owner, device, own in place.owner_peers():
        yield 0, slots.at[owner], outs[0].at[place.owner], device, own, None, own


def collect(place, ins, outs):
    slots, query, output, hidden, attended = ins
    tokens = query.shape[0] // place.fars
    depth = hidden.shape[1]
    each = place.fars // place.mps
    for far, device, own in place.far_peers():
        for group, values in ((1, query), (2, output)):
            target = block(outs[group], place.far, tokens)
            yield group, block(values, far, tokens), target, device, own, None, own
    mp, at = place.far // each, lax.rem(place.far, each)
    for step, (far, _, own) in enumerate(place.far_peers()):
        absent = place.skips(step)
        mine = mp == place.mp if own else False
        for group, values in ((3, hidden), (4, attended)):
            target = outs[group].at[
                pl.ds(pl.multiple_of(place.mp * tokens, tokens), tokens),
                pl.ds(pl.multiple_of(at * depth, depth), depth),
            ]
            device, lane = (far, place.near, mp), place.mp * each + at
            yield group, block(values, far, tokens), target, device, mine, lane, absent
    for owner, device, own in place.owner_peers():
        yield 0, slots.at[owner], outs[0].at[place.owner], device, own, None, own


def on_device(
    hidden,
    attended,
    query_cotangent,
    output_cotangent,
    query_projection_weight,
    output_projection_weight,
    narrower,
    widener,
    reducer,
    enlarger,
    block_adapter,
    block_fill,
):
    far = lax.axis_size("far")
    owners = far * lax.axis_size("near")
    tokens = hidden.shape[0]
    group_blocks = block_adapter.shape[0]
    width = tokens // group_blocks
    capacity = -(-group_blocks // owners)
    per_owner, rank = narrower.shape[:2]
    lanes = -(-per_owner // 128) * 128

    row_ids = iota((group_blocks, width), 1)
    live = one_hot(row_ids < block_fill[:, None]).reshape(tokens, 1)
    query_masked = query_cotangent * live
    output_masked = output_cotangent * live

    owner_of = block_adapter // per_owner
    later_ids = iota((group_blocks, group_blocks), 0)
    earlier_ids = iota((group_blocks, group_blocks), 1)
    before = (owner_of[:, None] == owner_of[None, :]) & (earlier_ids < later_ids)
    position = jnp.sum(before.astype(jnp.int32), axis=1)
    slot_of = owner_of * capacity + position
    row_of = (slot_of[:, None] * width + row_ids).reshape(1, tokens)
    table = one_hot(iota((owners * capacity * width, tokens), 0) == row_of)
    local_of = jnp.broadcast_to((block_adapter % per_owner)[:, None], (group_blocks, width))
    local_hot = one_hot(iota((tokens, lanes), 1) == local_of.reshape(tokens, 1))
    sent = jnp.concatenate(
        [
            product(table, part, (1, 0)).astype(jnp.bfloat16)
            for part in (local_hot, hidden, attended, query_masked, output_masked)
        ],
        axis=1,
    )
    model, query = hidden.shape[1], attended.shape[1]
    ends = [lanes, lanes + model, lanes + model + query, lanes + model + 2 * query]
    near, mps = lax.axis_size("near"), lax.axis_size("mp")
    depth = model * mps // far
    depth_out = query * mps // far
    high, wide = query_projection_weight.shape
    high_out, wide_out = output_projection_weight.shape
    slots = (owners, capacity * width, sent.shape[1])
    received, query_rows, output_rows, inputs, inputs_out, qcots, ocots = transfer(
        distribute,
        (
            sent.reshape(slots),
            query_projection_weight,
            output_projection_weight,
            hidden,
            attended,
            query_masked,
            output_masked,
        ),
        (
            slots,
            (near * high, wide),
            (near * high_out, wide_out),
            (far * tokens, depth),
            (far * tokens, depth_out),
            (far * tokens, wide),
            (far * tokens, wide_out),
        ),
        (
            slots[1:],
            (high, wide),
            (high_out, wide_out),
            (tokens, depth),
            (tokens, depth_out),
            (tokens, wide),
            (tokens, wide_out),
        ),
        2 * near + 4 * far + owners,
        0,
    )
    received = received.reshape(sent.shape)
    hot, hid, att, qcot, ocot = jnp.split(received, ends, axis=1)

    many = per_owner * rank
    spread = one_hot(iota((lanes, many), 0) == iota((lanes, many), 1) // rank)
    own = product(hot, spread, (1, 0))
    fold = one_hot(iota((many, rank), 0) % rank == iota((many, rank), 1))
    factors = [f.reshape(many, f.shape[2]) for f in (narrower, reducer, widener, enlarger)]
    folded = jnp.concatenate(
        [
            product((product(x, f, (1, 1)) * own).astype(jnp.bfloat16), fold, (1, 0))
            for x, f in zip((hid, att, qcot, ocot), factors)
        ],
        axis=1,
    ).astype(jnp.bfloat16)
    ranks = lax.psum(folded, "mp")
    query_rank, output_rank, query_back, output_back = [
        (product(ranks[:, i * rank : (i + 1) * rank], fold, (1, 1)) * own).astype(jnp.bfloat16)
        for i in range(4)
    ]
    down_query, down_output, up_query, up_output = factors
    lifted = jnp.concatenate(
        [
            (adapter_scale * product(r, f, (1, 0))).astype(jnp.bfloat16)
            for r, f in (
                (query_rank, up_query),
                (output_rank, up_output),
                (query_back, down_query),
                (output_back, down_output),
            )
        ],
        axis=1,
    )

    def gradient(ranks, rows, like):
        return (adapter_scale * product(ranks, rows, (0, 0))).reshape(like.shape)

    narrower_gradient = gradient(query_back, hid, narrower)
    widener_gradient = gradient(query_rank, qcot, widener)
    reducer_gradient = gradient(output_back, att, reducer)
    enlarger_gradient = gradient(output_rank, ocot, enlarger)

    parts = [
        product(values, weight, contract).astype(jnp.bfloat16)
        for values, weight, contract in (
            (inputs, query_rows, (1, 0)),
            (inputs_out, output_rows, (1, 0)),
            (qcots, query_rows, (1, 1)),
            (ocots, output_rows, (1, 1)),
        )
    ]
    slots = (owners, capacity * width, lifted.shape[1])
    returned, *terms = transfer(
        collect,
        (lifted.reshape(slots), *parts),
        (
            slots,
            (far * tokens, wide),
            (far * tokens, wide_out),
            (mps * tokens, model),
            (mps * tokens, query),
        ),
        (
            slots[1:],
            (tokens, wide),
            (tokens, wide_out),
            (tokens, depth),
            (tokens, depth_out),
        ),
        4 * far + owners,
        1,
    )
    returned = returned.reshape(lifted.shape)
    base = [
        jnp.sum(term.reshape(-1, tokens, term.shape[1]).astype(jnp.float32), axis=0)
        for term in terms
    ]
    starts = [query, query + model, query + 2 * model]
    adapter_terms = [product(table, part, (0, 0)) for part in jnp.split(returned, starts, axis=1)]
    queries, projected, hidden_state_gradient, attention_output_gradient = [
        (b + t).astype(jnp.bfloat16) for b, t in zip(base, adapter_terms)
    ]
    return (
        queries,
        projected,
        hidden_state_gradient,
        attention_output_gradient,
        narrower_gradient,
        widener_gradient,
        reducer_gradient,
        enlarger_gradient,
    )


def solution(mesh):
    count = mesh.shape["dp"]
    far = 1
    while far * far < count or count % far or far % mesh.shape["mp"]:
        far += 1
    split = Mesh(
        mesh.devices.reshape(far, count // far, mesh.shape["mp"]), ("far", "near", "mp")
    )
    dp = ("far", "near")
    rows, factors = P(dp, "mp"), P(dp, None, "mp")
    return jax.shard_map(
        on_device,
        mesh=split,
        in_specs=(rows,) * 6 + (factors,) * 4 + (P(dp),) * 2,
        out_specs=(rows,) * 4 + (factors,) * 4,
        check_vma=False,
    )
```

```python
import jax
import jax.numpy as jnp
from jax import lax
from jax.experimental import pallas as pl
from jax.experimental.pallas import tpu as pltpu
from jax.sharding import Mesh, PartitionSpec as P

adapter_scale = 2.0


def product(left, right, contract):
    return lax.dot_general(
        left, right, ((contract[:1], contract[1:]), ((), ())), preferred_element_type=jnp.float32
    )


def one_hot(condition):
    return condition.astype(jnp.bfloat16)


def iota(shape, dimension):
    return lax.broadcasted_iota(jnp.int32, shape, dimension)


def block(ref, index, rows):
    return ref.at[pl.ds(pl.multiple_of(index * rows, rows), rows)]


class Place:
    def __init__(self):
        names = ("top", "far", "low", "mp")
        self.top, self.far, self.low, self.mp = [lax.axis_index(name) for name in names]
        self.tops, self.fars, self.lows, self.mps = [lax.axis_size(name) for name in names]
        self.near, self.nears = self.top * self.lows + self.low, self.tops * self.lows
        self.owner = (self.top * self.fars + self.far) * self.lows + self.low
        self.owners = self.fars * self.nears

    def near_peers(self):
        for step in range(self.nears):
            near = lax.rem(self.near + step, self.nears)
            device = (near // self.lows, self.far, lax.rem(near, self.lows), self.mp)
            yield near, device, step == 0

    def far_peers(self):
        for step in range(self.fars):
            far = lax.rem(self.far + step, self.fars)
            yield far, (self.top, far, self.low, self.mp), step == 0

    def owner_peers(self):
        for step in range(self.owners):
            owner = lax.rem(self.owner + step, self.owners)
            rest = owner // self.lows
            top, far, low = rest // self.fars, lax.rem(rest, self.fars), lax.rem(owner, self.lows)
            yield owner, (top, far, low, self.mp), step == 0

    def feature_peers(self):
        each = self.tops // self.mps
        for far, _, own in self.far_peers():
            for shift in range(self.mps):
                mp = lax.rem(self.mp + shift, self.mps)
                for at in range(each):
                    device = (self.top, far, self.low, mp)
                    yield far, mp, at, device, own and shift == 0

    def greet(self):
        others = [device for _, device, own in self.owner_peers() if not own]
        for shift in range(1, self.mps):
            mp = lax.rem(self.mp + shift, self.mps)
            others += [(self.top, far, self.low, mp) for far in range(self.fars)]
        barrier = pltpu.get_barrier_semaphore()
        for device in others:
            pl.semaphore_signal(
                barrier, inc=1, device_id=device, device_id_type=pl.DeviceIdType.MESH
            )
        pl.semaphore_wait(barrier, len(others))


def columns_of(ref, rows, start, columns):
    return ref.at[rows, pl.ds(pl.multiple_of(start, columns), columns)]


def transfer(plan, arrays, out_shapes, chunks, sends, collective_id):
    count, groups = len(arrays), len(chunks)

    def kernel(*refs):
        ins, outs = refs[:count], refs[count : count + groups]
        held = refs[count + groups : count + 2 * groups]
        send_sem, recv_sem, own_sem = refs[count + 2 * groups :]
        place = Place()
        place.greet()
        routes = list(plan(place, ins, outs))

        owned = [0] * groups
        copies, passing = [], []
        for at, (group, source, target, device, own) in enumerate(routes):
            if own:
                keep, sem = held[group].at[owned[group]], own_sem.at[len(passing)]
                owned[group] += 1
                inward = pltpu.make_async_copy(source, keep, sem)
                passing.append((inward, pltpu.make_async_copy(keep, target, sem)))
                continue
            copies.append(
                pltpu.make_async_remote_copy(
                    src_ref=source,
                    dst_ref=target,
                    send_sem=send_sem.at[at],
                    recv_sem=recv_sem.at[at],
                    device_id=device,
                    device_id_type=pl.DeviceIdType.MESH,
                )
            )
        for copy in copies:
            copy.start()
        for inward, _ in passing:
            inward.start()
        for inward, outward in passing:
            inward.wait()
            outward.start()
        for _, outward in passing:
            outward.wait()
        for copy in copies:
            copy.wait()

    anywhere = pl.BlockSpec(memory_space=pl.ANY)
    return pl.pallas_call(
        kernel,
        out_shape=[jax.ShapeDtypeStruct(shape, jnp.bfloat16) for shape in out_shapes],
        in_specs=[anywhere] * count,
        out_specs=[anywhere] * groups,
        scratch_shapes=[pltpu.VMEM(shape, jnp.bfloat16) for shape in chunks]
        + [pltpu.SemaphoreType.DMA((sends,))] * 2
        + [pltpu.SemaphoreType.DMA((sum(shape[0] for shape in chunks),))],
        compiler_params=pltpu.CompilerParams(
            collective_id=collective_id, has_side_effects=True
        ),
    )(*arrays)


def distribute(place, ins, outs):
    slots, first, second, hidden, attended, query, output = ins
    tokens = hidden.shape[0]
    each = place.tops // place.mps
    for near, device, own in place.near_peers():
        for group, weight in ((1, first), (2, second)):
            rows = weight.shape[0]
            yield group, weight, block(outs[group], place.near, rows), device, own
    for far, mp, at, device, own in place.feature_peers():
        for group, values in ((3, hidden), (4, attended)):
            high = outs[group].shape[1] // place.tops
            source = columns_of(values, slice(None), (at * place.fars + far) * high, high)
            rows = pl.ds(pl.multiple_of(place.far * tokens, tokens), tokens)
            target = columns_of(outs[group], rows, (place.mp * each + at) * high, high)
            yield group, source, target, device, own
    for far, device, own in place.far_peers():
        for group, values in ((5, query), (6, output)):
            yield group, values, block(outs[group], place.far, tokens), device, own
    for owner, device, own in place.owner_peers():
        yield 0, slots.at[owner], outs[0].at[place.owner], device, own


def collect(place, ins, outs):
    slots, query, output, hidden, attended = ins
    tokens = query.shape[0] // place.fars
    each = place.tops // place.mps
    for far, device, own in place.far_peers():
        for group, values in ((1, query), (2, output)):
            target = block(outs[group], place.far, tokens)
            yield group, block(values, far, tokens), target, device, own
    for far, mp, at, device, own in place.feature_peers():
        for group, values in ((3, hidden), (4, attended)):
            high = values.shape[1] // place.tops
            rows = pl.ds(pl.multiple_of(far * tokens, tokens), tokens)
            source = columns_of(values, rows, (mp * each + at) * high, high)
            rows = pl.ds(pl.multiple_of(place.mp * tokens, tokens), tokens)
            target = columns_of(outs[group], rows, (at * place.fars + place.far) * high, high)
            yield group, source, target, device, own
    for owner, device, own in place.owner_peers():
        yield 0, slots.at[owner], outs[0].at[place.owner], device, own


def on_device(
    hidden,
    attended,
    query_cotangent,
    output_cotangent,
    query_projection_weight,
    output_projection_weight,
    narrower,
    widener,
    reducer,
    enlarger,
    block_adapter,
    block_fill,
):
    far = lax.axis_size("far")
    owners = far * lax.axis_size("top") * lax.axis_size("low")
    tokens = hidden.shape[0]
    group_blocks = block_adapter.shape[0]
    width = tokens // group_blocks
    capacity = -(-group_blocks // owners)
    per_owner, rank = narrower.shape[:2]
    lanes = -(-per_owner // 128) * 128

    row_ids = iota((group_blocks, width), 1)
    live = one_hot(row_ids < block_fill[:, None]).reshape(tokens, 1)
    query_masked = query_cotangent * live
    output_masked = output_cotangent * live

    owner_of = block_adapter // per_owner
    later_ids = iota((group_blocks, group_blocks), 0)
    earlier_ids = iota((group_blocks, group_blocks), 1)
    before = (owner_of[:, None] == owner_of[None, :]) & (earlier_ids < later_ids)
    position = jnp.sum(before.astype(jnp.int32), axis=1)
    slot_of = owner_of * capacity + position
    row_of = (slot_of[:, None] * width + row_ids).reshape(1, tokens)
    table = one_hot(iota((owners * capacity * width, tokens), 0) == row_of)
    local_of = jnp.broadcast_to((block_adapter % per_owner)[:, None], (group_blocks, width))
    local_hot = one_hot(iota((tokens, lanes), 1) == local_of.reshape(tokens, 1))
    sent = jnp.concatenate(
        [
            product(table, part, (1, 0)).astype(jnp.bfloat16)
            for part in (local_hot, hidden, attended, query_masked, output_masked)
        ],
        axis=1,
    )
    model, query = hidden.shape[1], attended.shape[1]
    ends = [lanes, lanes + model, lanes + model + query, lanes + model + 2 * query]
    lows, mps = lax.axis_size("low"), lax.axis_size("mp")
    near = lax.axis_size("top") * lows
    each = lax.axis_size("top") // mps
    depth = model * mps // far
    depth_out = query * mps // far
    high, wide = query_projection_weight.shape
    high_out, wide_out = output_projection_weight.shape
    slots = (owners, capacity * width, sent.shape[1])
    received, query_rows, output_rows, inputs, inputs_out, qcots, ocots = transfer(
        distribute,
        (
            sent.reshape(slots),
            query_projection_weight,
            output_projection_weight,
            hidden,
            attended,
            query_masked,
            output_masked,
        ),
        (
            slots,
            (near * high, wide),
            (near * high_out, wide_out),
            (far * tokens, depth),
            (far * tokens, depth_out),
            (far * tokens, wide),
            (far * tokens, wide_out),
        ),
        (
            (1, *slots[1:]),
            (1, high, wide),
            (1, high_out, wide_out),
            (each, tokens, lows * high),
            (each, tokens, lows * high_out),
            (1, tokens, wide),
            (1, tokens, wide_out),
        ),
        2 * near + 2 * far * mps * each + 2 * far + owners,
        0,
    )
    received = received.reshape(sent.shape)
    hot, hid, att, qcot, ocot = jnp.split(received, ends, axis=1)

    many = per_owner * rank
    spread = one_hot(iota((lanes, many), 0) == iota((lanes, many), 1) // rank)
    own = product(hot, spread, (1, 0))
    fold = one_hot(iota((many, rank), 0) % rank == iota((many, rank), 1))
    factors = [f.reshape(many, f.shape[2]) for f in (narrower, reducer, widener, enlarger)]
    folded = jnp.concatenate(
        [
            product((product(x, f, (1, 1)) * own).astype(jnp.bfloat16), fold, (1, 0))
            for x, f in zip((hid, att, qcot, ocot), factors)
        ],
        axis=1,
    ).astype(jnp.bfloat16)
    ranks = lax.psum(folded, "mp")
    query_rank, output_rank, query_back, output_back = [
        (product(ranks[:, i * rank : (i + 1) * rank], fold, (1, 1)) * own).astype(jnp.bfloat16)
        for i in range(4)
    ]
    down_query, down_output, up_query, up_output = factors
    lifted = jnp.concatenate(
        [
            (adapter_scale * product(r, f, (1, 0))).astype(jnp.bfloat16)
            for r, f in (
                (query_rank, up_query),
                (output_rank, up_output),
                (query_back, down_query),
                (output_back, down_output),
            )
        ],
        axis=1,
    )

    def gradient(ranks, rows, like):
        return (adapter_scale * product(ranks, rows, (0, 0))).reshape(like.shape)

    narrower_gradient = gradient(query_back, hid, narrower)
    widener_gradient = gradient(query_rank, qcot, widener)
    reducer_gradient = gradient(output_back, att, reducer)
    enlarger_gradient = gradient(output_rank, ocot, enlarger)

    parts = [
        product(values, weight, contract).astype(jnp.bfloat16)
        for values, weight, contract in (
            (inputs, query_rows, (1, 0)),
            (inputs_out, output_rows, (1, 0)),
            (qcots, query_rows, (1, 1)),
            (ocots, output_rows, (1, 1)),
        )
    ]
    slots = (owners, capacity * width, lifted.shape[1])
    returned, *terms = transfer(
        collect,
        (lifted.reshape(slots), *parts),
        (
            slots,
            (far * tokens, wide),
            (far * tokens, wide_out),
            (mps * tokens, model),
            (mps * tokens, query),
        ),
        (
            (1, *slots[1:]),
            (1, tokens, wide),
            (1, tokens, wide_out),
            (each, tokens, lows * high),
            (each, tokens, lows * high_out),
        ),
        2 * far + 2 * far * mps * each + owners,
        1,
    )
    returned = returned.reshape(lifted.shape)
    base = [
        jnp.sum(term.reshape(-1, tokens, term.shape[1]).astype(jnp.float32), axis=0)
        for term in terms
    ]
    starts = [query, query + model, query + 2 * model]
    adapter_terms = [product(table, part, (0, 0)) for part in jnp.split(returned, starts, axis=1)]
    queries, projected, hidden_state_gradient, attention_output_gradient = [
        (b + t).astype(jnp.bfloat16) for b, t in zip(base, adapter_terms)
    ]
    return (
        queries,
        projected,
        hidden_state_gradient,
        attention_output_gradient,
        narrower_gradient,
        widener_gradient,
        reducer_gradient,
        enlarger_gradient,
    )


def solution(mesh):
    count, mps = mesh.shape["dp"], mesh.shape["mp"]

    def on_split(*arrays):
        low = 1
        while arrays[4].shape[0] // count * low % 128:
            low += 1
        top = 1
        while top * top * low < count // low or count % (top * low) or top % mps:
            top += 1
        return build(mesh, top, low)(*arrays)

    return on_split


def build(mesh, top, low):
    shape = (top, mesh.shape["dp"] // (top * low), low, mesh.shape["mp"])
    split = Mesh(mesh.devices.reshape(shape), ("top", "far", "low", "mp"))
    dp = ("top", "far", "low")
    rows, factors = P(dp, "mp"), P(dp, None, "mp")
    return jax.shard_map(
        on_device,
        mesh=split,
        in_specs=(rows,) * 6 + (factors,) * 4 + (P(dp),) * 2,
        out_specs=(rows,) * 4 + (factors,) * 4,
        check_vma=False,
    )
```

```python
import jax
import jax.numpy as jnp
from jax import lax
from jax.experimental import pallas as pl
from jax.experimental.pallas import tpu as pltpu
from jax.sharding import Mesh, PartitionSpec as P

adapter_scale = 2.0


def product(left, right, contract):
    return lax.dot_general(
        left, right, ((contract[:1], contract[1:]), ((), ())), preferred_element_type=jnp.float32
    )


def one_hot(condition):
    return condition.astype(jnp.bfloat16)


def iota(shape, dimension):
    return lax.broadcasted_iota(jnp.int32, shape, dimension)


def block(ref, index, rows):
    return ref.at[pl.ds(pl.multiple_of(index * rows, rows), rows)]


class Place:
    def __init__(self):
        names = ("top", "far", "low", "mp")
        self.top, self.far, self.low, self.mp = [lax.axis_index(name) for name in names]
        self.tops, self.fars, self.lows, self.mps = [lax.axis_size(name) for name in names]
        self.near, self.nears = self.top * self.lows + self.low, self.tops * self.lows
        self.owner = (self.top * self.fars + self.far) * self.lows + self.low
        self.owners = self.fars * self.nears

    def near_peers(self):
        for step in range(self.nears):
            near = lax.rem(self.near + step, self.nears)
            device = (near // self.lows, self.far, lax.rem(near, self.lows), self.mp)
            yield near, device, step == 0

    def far_peers(self):
        for step in range(self.fars):
            far = lax.rem(self.far + step, self.fars)
            yield far, (self.top, far, self.low, self.mp), step == 0

    def owner_peers(self):
        for step in range(self.owners):
            owner = lax.rem(self.owner + step, self.owners)
            rest = owner // self.lows
            top, far, low = rest // self.fars, lax.rem(rest, self.fars), lax.rem(owner, self.lows)
            yield owner, (top, far, low, self.mp), step == 0

    def feature_peers(self):
        each = self.tops // self.mps
        for far, _, own in self.far_peers():
            for shift in range(self.mps):
                mp = lax.rem(self.mp + shift, self.mps)
                for at in range(each):
                    device = (self.top, far, self.low, mp)
                    yield far, mp, at, device, own and shift == 0

    def greet(self):
        others = [device for _, device, own in self.owner_peers() if not own]
        for shift in range(1, self.mps):
            mp = lax.rem(self.mp + shift, self.mps)
            others += [(self.top, far, self.low, mp) for far in range(self.fars)]
        barrier = pltpu.get_barrier_semaphore()
        for device in others:
            pl.semaphore_signal(
                barrier, inc=1, device_id=device, device_id_type=pl.DeviceIdType.MESH
            )
        pl.semaphore_wait(barrier, len(others))


def columns_of(ref, rows, start, columns):
    return ref.at[rows, pl.ds(pl.multiple_of(start, columns), columns)]


def relay(place, ins, outs, groups, send_sem, recv_sem):
    last = place.nears - 1

    def within(near):
        return jnp.logical_and(near >= 0, near <= last)

    def hop(step, way, group):
        shard = jnp.clip(place.near - way * (step - 1), 0, last)
        target = block(outs[group], shard, ins[group].shape[0])
        to = jnp.clip(place.near + way, 0, last)
        at = ((step - 1) * 2 + (way > 0)) * len(groups) + groups.index(group)
        return pltpu.make_async_remote_copy(
            src_ref=ins[group] if step == 1 else target,
            dst_ref=target,
            send_sem=send_sem.at[at],
            recv_sem=recv_sem.at[at],
            device_id=(to // place.lows, place.far, lax.rem(to, place.lows), place.mp),
            device_id_type=pl.DeviceIdType.MESH,
        )

    def sends(step, way):
        ahead = within(place.near + way)
        return jnp.logical_and(ahead, within(place.near - way * (step - 1)))

    every = [(way, group) for group in groups for way in (1, -1)]
    for step in range(1, place.nears + 1):
        for way, group in every:
            if step > 1:
                arrives = within(place.near - way * (step - 1))
                pl.when(arrives)(lambda: hop(step - 1, way, group).wait_recv())
            if step <= last:
                pl.when(sends(step, way))(lambda: hop(step, way, group).start())
    for step in range(1, place.nears):
        for way, group in every:
            pl.when(sends(step, way))(lambda: hop(step, way, group).wait_send())


def transfer(plan, arrays, out_shapes, chunks, sends, collective_id, relayed=(), links=0):
    count, groups = len(arrays), len(chunks)

    def kernel(*refs):
        ins, outs = refs[:count], refs[count : count + groups]
        held = refs[count + groups : count + 2 * groups]
        send_sem, recv_sem, own_sem, chain_send, chain_recv = refs[count + 2 * groups :]
        place = Place()
        place.greet()
        routes = list(plan(place, ins, outs))

        owned = [0] * groups
        copies, passing = [], []
        for at, (group, source, target, device, own) in enumerate(routes):
            if own:
                keep, sem = held[group].at[owned[group]], own_sem.at[len(passing)]
                owned[group] += 1
                inward = pltpu.make_async_copy(source, keep, sem)
                passing.append((inward, pltpu.make_async_copy(keep, target, sem)))
                continue
            copies.append(
                pltpu.make_async_remote_copy(
                    src_ref=source,
                    dst_ref=target,
                    send_sem=send_sem.at[at],
                    recv_sem=recv_sem.at[at],
                    device_id=device,
                    device_id_type=pl.DeviceIdType.MESH,
                )
            )
        for copy in copies:
            copy.start()
        for inward, _ in passing:
            inward.start()
        if relayed:
            relay(place, ins, outs, relayed, chain_send, chain_recv)
        for inward, outward in passing:
            inward.wait()
            outward.start()
        for _, outward in passing:
            outward.wait()
        for copy in copies:
            copy.wait()

    anywhere = pl.BlockSpec(memory_space=pl.ANY)
    return pl.pallas_call(
        kernel,
        out_shape=[jax.ShapeDtypeStruct(shape, jnp.bfloat16) for shape in out_shapes],
        in_specs=[anywhere] * count,
        out_specs=[anywhere] * groups,
        scratch_shapes=[pltpu.VMEM(shape, jnp.bfloat16) for shape in chunks]
        + [pltpu.SemaphoreType.DMA((sends,))] * 2
        + [pltpu.SemaphoreType.DMA((sum(shape[0] for shape in chunks),))]
        + [pltpu.SemaphoreType.DMA((max(links, 1),))] * 2,
        compiler_params=pltpu.CompilerParams(
            collective_id=collective_id, has_side_effects=True
        ),
    )(*arrays)


def distribute(place, ins, outs):
    slots, first, second, hidden, attended, query, output = ins
    tokens = hidden.shape[0]
    each = place.tops // place.mps
    for near, device, own in place.near_peers():
        for group, weight in ((1, first), (2, second)):
            rows = weight.shape[0]
            if own:
                yield group, weight, block(outs[group], place.near, rows), device, own
    for far, mp, at, device, own in place.feature_peers():
        for group, values in ((3, hidden), (4, attended)):
            high = outs[group].shape[1] // place.tops
            source = columns_of(values, slice(None), (at * place.fars + far) * high, high)
            rows = pl.ds(pl.multiple_of(place.far * tokens, tokens), tokens)
            target = columns_of(outs[group], rows, (place.mp * each + at) * high, high)
            yield group, source, target, device, own
    for far, device, own in place.far_peers():
        for group, values in ((5, query), (6, output)):
            yield group, values, block(outs[group], place.far, tokens), device, own
    for owner, device, own in place.owner_peers():
        yield 0, slots.at[owner], outs[0].at[place.owner], device, own


def collect(place, ins, outs):
    slots, query, output, hidden, attended = ins
    tokens = query.shape[0] // place.fars
    each = place.tops // place.mps
    for far, device, own in place.far_peers():
        for group, values in ((1, query), (2, output)):
            target = block(outs[group], place.far, tokens)
            yield group, block(values, far, tokens), target, device, own
    for far, mp, at, device, own in place.feature_peers():
        for group, values in ((3, hidden), (4, attended)):
            high = values.shape[1] // place.tops
            rows = pl.ds(pl.multiple_of(far * tokens, tokens), tokens)
            source = columns_of(values, rows, (mp * each + at) * high, high)
            rows = pl.ds(pl.multiple_of(place.mp * tokens, tokens), tokens)
            target = columns_of(outs[group], rows, (at * place.fars + place.far) * high, high)
            yield group, source, target, device, own
    for owner, device, own in place.owner_peers():
        yield 0, slots.at[owner], outs[0].at[place.owner], device, own


def on_device(
    hidden,
    attended,
    query_cotangent,
    output_cotangent,
    query_projection_weight,
    output_projection_weight,
    narrower,
    widener,
    reducer,
    enlarger,
    block_adapter,
    block_fill,
):
    far = lax.axis_size("far")
    owners = far * lax.axis_size("top") * lax.axis_size("low")
    tokens = hidden.shape[0]
    group_blocks = block_adapter.shape[0]
    width = tokens // group_blocks
    capacity = -(-group_blocks // owners)
    per_owner, rank = narrower.shape[:2]
    lanes = -(-per_owner // 128) * 128

    row_ids = iota((group_blocks, width), 1)
    live = one_hot(row_ids < block_fill[:, None]).reshape(tokens, 1)
    query_masked = query_cotangent * live
    output_masked = output_cotangent * live

    owner_of = block_adapter // per_owner
    later_ids = iota((group_blocks, group_blocks), 0)
    earlier_ids = iota((group_blocks, group_blocks), 1)
    before = (owner_of[:, None] == owner_of[None, :]) & (earlier_ids < later_ids)
    position = jnp.sum(before.astype(jnp.int32), axis=1)
    slot_of = owner_of * capacity + position
    row_of = (slot_of[:, None] * width + row_ids).reshape(1, tokens)
    table = one_hot(iota((owners * capacity * width, tokens), 0) == row_of)
    local_of = jnp.broadcast_to((block_adapter % per_owner)[:, None], (group_blocks, width))
    local_hot = one_hot(iota((tokens, lanes), 1) == local_of.reshape(tokens, 1))
    sent = jnp.concatenate(
        [
            product(table, part, (1, 0)).astype(jnp.bfloat16)
            for part in (local_hot, hidden, attended, query_masked, output_masked)
        ],
        axis=1,
    )
    model, query = hidden.shape[1], attended.shape[1]
    ends = [lanes, lanes + model, lanes + model + query, lanes + model + 2 * query]
    lows, mps = lax.axis_size("low"), lax.axis_size("mp")
    near = lax.axis_size("top") * lows
    each = lax.axis_size("top") // mps
    depth = model * mps // far
    depth_out = query * mps // far
    high, wide = query_projection_weight.shape
    high_out, wide_out = output_projection_weight.shape
    slots = (owners, capacity * width, sent.shape[1])
    received, query_rows, output_rows, inputs, inputs_out, qcots, ocots = transfer(
        distribute,
        (
            sent.reshape(slots),
            query_projection_weight,
            output_projection_weight,
            hidden,
            attended,
            query_masked,
            output_masked,
        ),
        (
            slots,
            (near * high, wide),
            (near * high_out, wide_out),
            (far * tokens, depth),
            (far * tokens, depth_out),
            (far * tokens, wide),
            (far * tokens, wide_out),
        ),
        (
            (1, *slots[1:]),
            (1, high, wide),
            (1, high_out, wide_out),
            (each, tokens, lows * high),
            (each, tokens, lows * high_out),
            (1, tokens, wide),
            (1, tokens, wide_out),
        ),
        2 * near + 2 * far * mps * each + 2 * far + owners,
        0,
        relayed=(1, 2),
        links=4 * (near - 1),
    )
    received = received.reshape(sent.shape)
    hot, hid, att, qcot, ocot = jnp.split(received, ends, axis=1)

    many = per_owner * rank
    spread = one_hot(iota((lanes, many), 0) == iota((lanes, many), 1) // rank)
    own = product(hot, spread, (1, 0))
    fold = one_hot(iota((many, rank), 0) % rank == iota((many, rank), 1))
    factors = [f.reshape(many, f.shape[2]) for f in (narrower, reducer, widener, enlarger)]
    folded = jnp.concatenate(
        [
            product((product(x, f, (1, 1)) * own).astype(jnp.bfloat16), fold, (1, 0))
            for x, f in zip((hid, att, qcot, ocot), factors)
        ],
        axis=1,
    ).astype(jnp.bfloat16)
    ranks = lax.psum(folded, "mp")
    query_rank, output_rank, query_back, output_back = [
        (product(ranks[:, i * rank : (i + 1) * rank], fold, (1, 1)) * own).astype(jnp.bfloat16)
        for i in range(4)
    ]
    down_query, down_output, up_query, up_output = factors
    lifted = jnp.concatenate(
        [
            (adapter_scale * product(r, f, (1, 0))).astype(jnp.bfloat16)
            for r, f in (
                (query_rank, up_query),
                (output_rank, up_output),
                (query_back, down_query),
                (output_back, down_output),
            )
        ],
        axis=1,
    )

    def gradient(ranks, rows, like):
        return (adapter_scale * product(ranks, rows, (0, 0))).reshape(like.shape)

    narrower_gradient = gradient(query_back, hid, narrower)
    widener_gradient = gradient(query_rank, qcot, widener)
    reducer_gradient = gradient(output_back, att, reducer)
    enlarger_gradient = gradient(output_rank, ocot, enlarger)

    parts = [
        product(values, weight, contract).astype(jnp.bfloat16)
        for values, weight, contract in (
            (inputs, query_rows, (1, 0)),
            (inputs_out, output_rows, (1, 0)),
            (qcots, query_rows, (1, 1)),
            (ocots, output_rows, (1, 1)),
        )
    ]
    slots = (owners, capacity * width, lifted.shape[1])
    returned, *terms = transfer(
        collect,
        (lifted.reshape(slots), *parts),
        (
            slots,
            (far * tokens, wide),
            (far * tokens, wide_out),
            (mps * tokens, model),
            (mps * tokens, query),
        ),
        (
            (1, *slots[1:]),
            (1, tokens, wide),
            (1, tokens, wide_out),
            (each, tokens, lows * high),
            (each, tokens, lows * high_out),
        ),
        2 * far + 2 * far * mps * each + owners,
        1,
    )
    returned = returned.reshape(lifted.shape)
    base = [
        jnp.sum(term.reshape(-1, tokens, term.shape[1]).astype(jnp.float32), axis=0)
        for term in terms
    ]
    starts = [query, query + model, query + 2 * model]
    adapter_terms = [product(table, part, (0, 0)) for part in jnp.split(returned, starts, axis=1)]
    queries, projected, hidden_state_gradient, attention_output_gradient = [
        (b + t).astype(jnp.bfloat16) for b, t in zip(base, adapter_terms)
    ]
    return (
        queries,
        projected,
        hidden_state_gradient,
        attention_output_gradient,
        narrower_gradient,
        widener_gradient,
        reducer_gradient,
        enlarger_gradient,
    )


def solution(mesh):
    count, mps = mesh.shape["dp"], mesh.shape["mp"]

    def on_split(*arrays):
        low = 1
        while arrays[4].shape[0] // count * low % 128:
            low += 1
        top = 1
        while top * top * low < count // low or count % (top * low) or top % mps:
            top += 1
        return build(mesh, top, low)(*arrays)

    return on_split


def build(mesh, top, low):
    shape = (top, mesh.shape["dp"] // (top * low), low, mesh.shape["mp"])
    split = Mesh(mesh.devices.reshape(shape), ("top", "far", "low", "mp"))
    dp = ("top", "far", "low")
    rows, factors = P(dp, "mp"), P(dp, None, "mp")
    return jax.shard_map(
        on_device,
        mesh=split,
        in_specs=(rows,) * 6 + (factors,) * 4 + (P(dp),) * 2,
        out_specs=(rows,) * 4 + (factors,) * 4,
        check_vma=False,
    )
```
